32 devices in a mesh: groups: 2 (over y), bx: 4 (over z), by: 2 (over x), bz: 2 (over core).
Axes of the slice: x: 2, y: 2, z: 4, core: 2. Of those that a mesh axis runs over, the one named last changes fastest.
Arguments:
- slab: float32 [4, 512, 1024], P(('groups', 'bz'), 'bx', 'by'), parts along dimension 0, may hold values from -6 to 6
- plane_test: float32 [2, 256], P('bz'), may hold values from -4 to 4
- row_test: float32 [512, 256], P('bx'), may hold values from -0.25 to 0.25
- col_test: float32 [1024, 256], P('by'), may hold values from -0.1875 to 0.1875
- core_planes: float32 [512, 2], P('bz'), may hold values from -4 to 4
- core_rows: float32 [512, 512], P(None, 'bx'), may hold values from -0.25 to 0.25
- core_cols: float32 [512, 1024], P(None, 'by'), may hold values from -0.1875 to 0.1875
Outputs:
- plane_sketch: float32 [4, 256], P(('groups', 'bz')), parts along dimension 0
- row_sketch: float32 [1024, 256], P(('groups', 'bx'), ('by', 'bz')), parts along dimension 0
- col_sketch: float32 [2048, 256], P(('groups', 'by'), ('bx', 'bz')), parts along dimension 0
- core_sketch: float32 [1024, 512, 512], P(('groups', 'bz'), 'bx', 'by'), parts along dimension 0
The draws below stay inside these ranges and needn't reach their ends.
There are 2 independent parts, one for each index of `groups`. The reference program is written for one: setup_inputs(seed, part) draws one part's arguments, and reference() takes and returns one part's arrays. A program takes and returns all parts, laid end to end along the dimension named above; an argument that names none is the same for every part. Nothing has to cross between parts.
All inputs are finite; a program needn't handle non-finite values.
Results may differ from the reference program's by a relative error of at most 0.00011.
Values sent between devices are 32-bit elements; how exact they have to be, the bound alone decides.
A program may use at most 128 MiB of HBM per device.

```python
import jax
import jax.numpy as jnp
from jax import lax

S = 512
K = 256
P_SIZE = 2
NR = 512
NC = 1024


def shard_levels(own_key, dims, pieces, smallest, top_value):
    level = 1.0
    for position, shards_of in pieces:
        heights = jax.random.uniform(jax.random.fold_in(jax.random.fold_in(own_key, 6), position), (shards_of,), jnp.float32, smallest / len(pieces), top_value / len(pieces))
        level = level * jnp.repeat(jnp.exp(heights), dims[position] // shards_of).reshape((-1,) + (1,) * (len(dims) - 1 - position))
    return level


def centred(rng, dims, spread, most, pieces=(), held_as=jnp.bfloat16):
    array = spread * jax.random.normal(rng, dims, jnp.float32)
    if pieces:
        array = array * shard_levels(rng, dims, pieces, -0.22, 0.18)
    return jnp.clip(array, -most, most).astype(held_as)


def setup_inputs(seed: int = 0, part: int = 0) -> dict:
    keys = jax.random.split(jax.random.key(seed), 8)
    part_keys = jax.random.split(jax.random.fold_in(keys[7], part), 8)
    return {
        "slab": centred(part_keys[0], (P_SIZE, NR, NC), 1.0, 6.0, ((0, 2), (1, 4), (2, 2)), jnp.float32),
        "plane_test": centred(keys[1], (P_SIZE, K), P_SIZE ** -0.5, 4.0, ((0, 2),), jnp.float32),
        "row_test": centred(keys[2], (NR, K), NR ** -0.5, 0.25, ((0, 4),), jnp.float32),
        "col_test": centred(keys[3], (NC, K), NC ** -0.5, 0.1875, ((0, 2),), jnp.float32),
        "core_planes": centred(keys[4], (S, P_SIZE), P_SIZE ** -0.5, 4.0, ((0, 2),), jnp.float32),
        "core_rows": centred(keys[5], (S, NR), NR ** -0.5, 0.25, ((1, 4),), jnp.float32),
        "core_cols": centred(keys[6], (S, NC), NC ** -0.5, 0.1875, ((1, 2),), jnp.float32),
    }


def reference(slab, plane_test, row_test, col_test, core_planes, core_rows, core_cols):
    highest = lax.Precision.HIGHEST
    by_col = jnp.einsum('pij,jr->pir', slab, col_test, precision=highest)
    plane_sketch = jnp.einsum('pir,ir->pr', by_col, row_test, precision=highest)
    row_sketch = jnp.einsum('pir,pr->ir', by_col, plane_test, precision=highest)
    by_row = jnp.einsum('pij,ir->pjr', slab, row_test, precision=highest)
    col_sketch = jnp.einsum('pjr,pr->jr', by_row, plane_test, precision=highest)
    shrunk = jnp.einsum('pij,bj->pib', slab, core_cols, precision=highest)
    partial_value = jnp.einsum('pib,ai->pab', shrunk, core_rows, precision=highest)
    core_sketch = jnp.einsum('cp,pab->cab', core_planes, partial_value, precision=highest)
    return plane_sketch, row_sketch, col_sketch, core_sketch
```

```python
import functools

import jax
import jax.numpy as jnp
from jax import lax
from jax.experimental import pallas as pl
from jax.experimental.pallas import tpu as pltpu
from jax.sharding import PartitionSpec as P

F32 = jnp.float32
MESH = pl.DeviceIdType.MESH


def split(x):
    high = x.astype(jnp.bfloat16)
    return high, (x - high.astype(F32)).astype(jnp.bfloat16)


def dot3(a, b, dims):
    f = functools.partial(
        lax.dot_general, dimension_numbers=(dims, ((), ())), preferred_element_type=F32
    )
    return f(a[0], b[0]) + (f(a[0], b[1]) + f(a[1], b[0]))


NN = ((1,), (0,))
NT = ((1,), (1,))


def exchange_kernel(
    nx, ny, nz,
    slab_hbm, plane_test_hbm, row_test_hbm, col_test_hbm, core_planes_hbm, core_rows_hbm, core_cols_hbm,
    *refs,
):
    gathered_ref, row_ref, plane_ref, planes_ref = refs[:4]
    col_ref = refs[4]
    (
        slab_ref, plane_test_ref, row_test_ref, col_test_ref, core_planes_ref, core_rows_ref, core_cols_ref,
        shrunk, shrunk_in, paired, part, part_in,
        row_a, row_a_in, row_b, row_b_in,
        col_a, col_a_in, col_b, col_b_in, col_c_in,
        plane_a, plane_a_in, plane_b, plane_b_in,
        send_sem, recv_sem, load_sem,
    ) = refs[5:]
    size = {"bx": nx, "by": ny, "bz": nz}
    me = {name: lax.axis_index(name) for name in size}
    odd, pair = lax.rem(me["bx"], 2), lax.div(me["bx"], 2)
    half = nx // 2
    count = [0]
    chunks, ni, wide = shrunk.shape[1:]
    tall = part.shape[2]

    loads = []

    def load(source, target):
        copy = pltpu.make_async_copy(source, target, load_sem.at[len(loads)])
        copy.start()
        loads.append(copy)
        return copy

    def cols_of(h):
        return [
            load(core_cols_hbm.at[pl.ds((y * chunks + h) * wide, wide)], core_cols_ref.at[h, pl.ds(y * wide, wide)])
            for y in range(ny)
        ]

    slab_load = [load(slab_hbm, slab_ref)]
    cols_load = [cols_of(0)]
    first_load = [load(row_test_hbm, row_test_ref), load(plane_test_hbm, plane_test_ref)]
    cols_load += [cols_of(h) for h in range(1, chunks)]
    rows_load = [load(core_rows_hbm.at[:, odd], core_rows_ref.at[:, :, pl.ds(0, ni)])]
    col_test_load = [load(col_test_hbm, col_test_ref)]
    planes_load = [load(core_planes_hbm, core_planes_ref)]

    def ready(group):
        for copy in group:
            copy.wait()

    def peer(name, d):
        return lax.rem(me[name] + d, size[name])

    barrier = pltpu.get_barrier_semaphore()
    for name in size:
        for d in range(1, size[name]):
            pl.semaphore_signal(barrier, inc=1, device_id={name: peer(name, d)}, device_id_type=MESH)

    copies = []

    def send(name, d, src, dst, to=None):
        n = count[0]
        count[0] += 1
        copy = pltpu.make_async_remote_copy(
            src_ref=src, dst_ref=dst, send_sem=send_sem.at[n], recv_sem=recv_sem.at[n],
            device_id={name: peer(name, d) if to is None else to}, device_id_type=MESH,
        )
        copy.start()
        copies.append(copy)
        return copy

    def send_all(name, source, landing):
        return [send(name, d, source(d), landing(d - 1)) for d in range(1, size[name])]

    def arrived(group):
        for copy in group:
            copy.wait_recv()

    partner = 2 * pair + 1 - odd

    ready(slab_load)
    ready(cols_load[0])
    slab = split(slab_ref[0])

    def shrink(h):
        terms = dot3(slab, split(core_cols_ref[h]), NT)
        for y in range(ny):
            shrunk[y, h] = terms[:, y * wide:(y + 1) * wide]

    def send_shrunk(h):
        return send_all("by", lambda d: shrunk.at[peer("by", d), h], lambda n: shrunk_in.at[n, h])

    shrink(0)
    pl.semaphore_wait(barrier, nx + ny + nz - 3)
    shrunk_sent = [send_shrunk(0)]
    rows_sent = send(
        "bx", 1, core_rows_hbm.at[:, 1 - odd], core_rows_ref.at[:, :, pl.ds(ni, ni)], to=partner
    )
    for h in range(1, chunks):
        ready(cols_load[h])
        shrink(h)
        shrunk_sent.append(send_shrunk(h))

    paired_sent = []

    def send_paired(h):
        arrived(shrunk_sent[h])
        total = shrunk[me["by"], h]
        for d in range(1, ny):
            total = total + shrunk_in[d - 1, h]
        paired[h, :ni] = total
        paired_sent.append(
            send("bx", 1, paired.at[h, pl.ds(0, ni)], paired.at[h, pl.ds(ni, ni)], to=partner)
        )

    ready(first_load)
    row_test = row_test_ref[...]
    plane_test = plane_test_ref[...]
    scaled = split((row_test * plane_test).T)
    terms = dot3(scaled, slab, NN)
    block = col_a.shape[3]
    for x in range(nx):
        for z in range(nz):
            first = (x * nz + z) * block
            col_a[z, x % 2, x // 2] = terms[first:first + block, :]
    col_a_sent = send_all("bz", lambda d: col_a.at[peer("bz", d)], lambda n: col_a_in.at[n])

    send_paired(0)

    ready(planes_load)
    for p in range(core_planes_ref.shape[0]):
        line = core_planes_ref[p:p + 1, :]
        planes_ref[p] = jnp.broadcast_to(line, (128, line.shape[1])).T

    ready(col_test_load)
    by_col = dot3(slab, split(col_test_ref[...]), NN)
    plane_a[...] = jnp.sum(by_col * row_test, axis=0, keepdims=True)
    plane_a_sent = send_all("by", lambda d: plane_a, lambda n: plane_a_in.at[n])
    terms = (by_col * plane_test).T
    block = row_a.shape[2]
    for y in range(ny):
        for z in range(nz):
            first = (y * nz + z) * block
            row_a[z, y] = terms[first:first + block, :]
    row_a_sent = send_all("bz", lambda d: row_a.at[peer("bz", d)], lambda n: row_a_in.at[n])

    for h in range(1, chunks):
        send_paired(h)

    ready(rows_load)
    rows_sent.wait_recv()
    part_sent = []

    def send_part(h):
        arrived([paired_sent[h]])
        reduced = split(paired[h])
        group = []
        for d in range(1, half + 1):
            to = lax.rem(pair + d, half)
            part[d - 1, h] = dot3(split(core_rows_ref[to]), reduced, NN)
            if d < half:
                group.append(send("bx", d, part.at[d - 1, h], part_in.at[d - 1, h], to=2 * to + odd))
        part_sent.append(group)

    send_part(0)

    arrived(col_a_sent)
    total = col_a[me["bz"]]
    for d in range(1, nz):
        total = total + col_a_in[d - 1]
    col_b[...] = total
    col_b_sent = send("bx", 1, col_b.at[1 - odd], col_b_in, to=partner)

    arrived(plane_a_sent)
    total = plane_a[...]
    for d in range(1, ny):
        total = total + plane_a_in[d - 1]
    plane_b[...] = total
    plane_b_sent = send_all("bx", lambda d: plane_b, lambda n: plane_b_in.at[n])

    arrived(row_a_sent)
    total = row_a[me["bz"]]
    for d in range(1, nz):
        total = total + row_a_in[d - 1]
    row_b[...] = total
    row_b_sent = send_all("by", lambda d: row_b.at[peer("by", d)], lambda n: row_b_in.at[n])

    for h in range(1, chunks):
        send_part(h)

    arrived([col_b_sent])
    col_b[odd] = col_b[odd] + col_b_in[...]
    col_c_sent = []
    for d in range(1, half):
        to = lax.rem(pair + d, half)
        col_c_sent.append(send("bx", d, col_b.at[odd, to], col_c_in.at[d - 1], to=2 * to + odd))

    def finish_part(h):
        total = part[half - 1, h]
        for d in range(1, half):
            part_sent[h][d - 1].wait_recv()
            total = total + part_in[d - 1, h]
        there = gathered_ref.at[me["bz"], h]
        there[...] = total
        return send_all("bz", lambda d: there, lambda n: there)

    full_sent = [finish_part(0)]

    arrived(row_b_sent)
    total = row_b[me["by"]]
    for d in range(1, ny):
        total = total + row_b_in[d - 1]
    row_ref[...] = total

    arrived(plane_b_sent)
    total = plane_b[...]
    for d in range(1, nx):
        total = total + plane_b_in[d - 1]
    plane_ref[...] = total

    for h in range(1, chunks):
        full_sent.append(finish_part(h))

    arrived(col_c_sent)
    total = col_b[odd, pair]
    for d in range(1, half):
        total = total + col_c_in[d - 1]
    col_ref[...] = total

    for group in full_sent:
        arrived(group)
    for copy in copies:
        copy.wait_send()


def core_kernel(
    planes_ref, gathered_ref, row_in, col_in, plane_in,
    row_ref, col_ref, plane_ref, out_ref,
    slots, out_sem, small_sem,
):
    count, rows = slots.shape[:2]
    steps = out_ref.shape[0] // rows
    planes, chunks, _, wide = gathered_ref.shape
    small = [
        pltpu.make_async_copy(source, target, small_sem.at[n])
        for n, (source, target) in enumerate(((row_in, row_ref), (col_in, col_ref), (plane_in, plane_ref)))
    ]

    def copy(step, slot):
        return pltpu.make_async_copy(
            slots.at[slot], out_ref.at[pl.ds(step * rows, rows)], out_sem.at[slot]
        )

    def body(step, _):
        slot = lax.rem(step, count)

        @pl.when(step >= count)
        def _():
            copy(step - count, slot).wait()

        for c in range(rows):
            row = step * rows + c
            value = [planes_ref[p, pl.ds(row, 1), :] for p in range(planes)]
            for h in range(chunks):
                total = value[0] * gathered_ref[0, h]
                for p in range(1, planes):
                    total = total + value[p] * gathered_ref[p, h]
                slots[slot, c, :, h * wide:(h + 1) * wide] = total
        copy(step, slot).start()
        return 0

    lax.fori_loop(0, steps, body, 0)
    for one in small:
        one.start()
    for step in range(steps - count, steps):
        copy(step, step % count).wait()
    for one in small:
        one.wait()


def on_device(nx, ny, nz, slab, plane_test, row_test, col_test, core_planes, core_rows, core_cols):
    rank = row_test.shape[1]
    ni, nj = slab.shape[1:]
    ab, bb = core_rows.shape[0] // nx, core_cols.shape[0] // ny
    rb, cb = rank // (ny * nz), rank // (nx * nz)
    half = nx // 2
    wide = 128
    chunks = bb // wide
    depth, planes = core_planes.shape
    shape = lambda *dims: jax.ShapeDtypeStruct(dims, F32)
    vmem = lambda *dims: pltpu.VMEM(dims, F32)
    inputs = (
        slab, plane_test, row_test, col_test, core_planes.T,
        core_rows.reshape(half, 2, ab, ni), core_cols,
    )
    transfers = 3 * (nz - 1) + chunks * (nz - 1) + (2 + chunks) * (ny - 1) + (nx - 1) + 2 + (1 + chunks) * half
    gathered, row_t, plane_sketch, planes_wide, col_t = pl.pallas_call(
        functools.partial(exchange_kernel, nx, ny, nz),
        out_shape=(
            shape(nz, chunks, ab, wide), shape(rb, ni), shape(1, rank), shape(planes, depth, 128),
            shape(cb, nj),
        ),
        in_specs=[pl.BlockSpec(memory_space=pltpu.HBM)] * 7,
        out_specs=[pl.BlockSpec(memory_space=pltpu.VMEM)] * 5,
        scratch_shapes=[
            vmem(1, ni, nj), vmem(1, rank), vmem(ni, rank), vmem(nj, rank), vmem(planes, depth),
            vmem(half, ab, 2 * ni), vmem(chunks, ny * wide, nj),
            vmem(ny, chunks, ni, wide), vmem(ny - 1, chunks, ni, wide),
            vmem(chunks, 2 * ni, wide),
            vmem(half, chunks, ab, wide), vmem(half - 1, chunks, ab, wide),
            vmem(nz, ny, rb, ni), vmem(nz - 1, ny, rb, ni),
            vmem(ny, rb, ni), vmem(ny - 1, rb, ni),
            vmem(nz, 2, half, cb, nj), vmem(nz - 1, 2, half, cb, nj),
            vmem(2, half, cb, nj), vmem(half, cb, nj), vmem(half - 1, cb, nj),
            vmem(1, rank), vmem(ny - 1, 1, rank),
            vmem(1, rank), vmem(nx - 1, 1, rank),
            pltpu.SemaphoreType.DMA((transfers,)),
            pltpu.SemaphoreType.DMA((transfers,)),
            pltpu.SemaphoreType.DMA((6 + chunks * ny,)),
        ],
        compiler_params=pltpu.CompilerParams(
            collective_id=0, has_side_effects=True, vmem_limit_bytes=32 << 20
        ),
        name="exchange",
    )(*(pltpu.with_memory_space_constraint(a, pltpu.HBM) for a in inputs))
    rows = min(depth, max(1, (1 << 17) // (ab * bb)))
    slots = min(8, depth // rows)
    row_t, col_t, plane_sketch, core_sketch = pl.pallas_call(
        core_kernel,
        out_shape=(shape(rb, ni), shape(cb, nj), shape(1, rank), shape(depth, ab, bb)),
        in_specs=[pl.BlockSpec(memory_space=pltpu.VMEM)] * 5,
        out_specs=[pl.BlockSpec(memory_space=pltpu.HBM)] * 4,
        scratch_shapes=[
            vmem(slots, rows, ab, bb),
            pltpu.SemaphoreType.DMA((slots,)),
            pltpu.SemaphoreType.DMA((3,)),
        ],
        compiler_params=pltpu.CompilerParams(vmem_limit_bytes=16 << 20),
        cost_estimate=pl.CostEstimate(flops=3 * depth * ab * bb, bytes_accessed=4 * depth * ab * bb, transcendentals=0),
        name="core",
    )(planes_wide, gathered, row_t, col_t, plane_sketch)
    return plane_sketch, row_t.T, col_t.T, core_sketch


def solution(mesh):
    in_specs = (
        P(("groups", "bz"), "bx", "by"),
        P("bz", None),
        P("bx", None),
        P("by", None),
        P("bz", None),
        P(None, "bx"),
        P(None, "by"),
    )
    out_specs = (
        P(("groups", "bz"), None),
        P(("groups", "bx"), ("by", "bz")),
        P(("groups", "by"), ("bx", "bz")),
        P(("groups", "bz"), "bx", "by"),
    )
    sizes = [mesh.shape[name] for name in ("bx", "by", "bz")]
    return jax.shard_map(
        functools.partial(on_device, *sizes),
        mesh=mesh, in_specs=in_specs, out_specs=out_specs, check_vma=False,
    )
```

```python
import functools

import jax
import jax.numpy as jnp
from jax import lax
from jax.experimental import pallas as pl
from jax.experimental.pallas import tpu as pltpu
from jax.sharding import PartitionSpec as P

F32 = jnp.float32
MESH = pl.DeviceIdType.MESH


def split(x):
    high = x.astype(jnp.bfloat16)
    return high, (x - high.astype(F32)).astype(jnp.bfloat16)


def dot3(a, b, dims):
    f = functools.partial(
        lax.dot_general, dimension_numbers=(dims, ((), ())), preferred_element_type=F32
    )
    return f(a[0], b[0]) + (f(a[0], b[1]) + f(a[1], b[0]))


NN = ((1,), (0,))
NT = ((1,), (1,))


PIECES = 2


def exchange_kernel(
    nx, ny, nz,
    slab_hbm, plane_test_hbm, row_test_hbm, col_test_hbm, core_planes_hbm, core_rows_hbm, core_cols_hbm,
    gathered_ref, row_ref, plane_ref, planes_ref, col_ref,
    slab_ref, plane_test_ref, row_test_ref, col_test_ref, core_planes_ref, core_rows_ref, core_cols_ref,
    shrunk, shrunk_in, held, part, part_in,
    row_a, row_a_in, row_b, row_b_in,
    col_a, col_a_in, col_b, col_b_in, col_c, col_c_in, col_near, col_near_in, col_far_in,
    plane_a, plane_a_in, plane_b, plane_b_in,
    send_sem, recv_sem, load_sem,
):
    size = {"bx": nx, "by": ny, "bz": nz}
    me = {name: lax.axis_index(name) for name in size}
    odd, pair = lax.rem(me["bx"], 2), lax.div(me["bx"], 2)
    half = nx // 2
    partner = 2 * pair + 1 - odd
    chunks, ni, wide = shrunk.shape[1:]

    loads = []

    def load(source, target):
        copy = pltpu.make_async_copy(source, target, load_sem.at[len(loads)])
        copy.start()
        loads.append(copy)
        return copy

    def cols_of(h):
        return [
            load(core_cols_hbm.at[pl.ds((y * chunks + h) * wide, wide)], core_cols_ref.at[h, pl.ds(y * wide, wide)])
            for y in range(ny)
        ]

    slab_load = [load(slab_hbm, slab_ref)]
    cols_load = [cols_of(0)]
    first_load = [load(row_test_hbm, row_test_ref), load(plane_test_hbm, plane_test_ref)]
    cols_load += [cols_of(h) for h in range(1, chunks)]

    def ready(group):
        for copy in group:
            copy.wait()

    def peer(name, d):
        return lax.rem(me[name] + d, size[name])

    barrier = pltpu.get_barrier_semaphore()
    for name in size:
        for d in range(1, size[name]):
            pl.semaphore_signal(barrier, inc=1, device_id={name: peer(name, d)}, device_id_type=MESH)

    pieces = [pl.ds(n * ni // PIECES, ni // PIECES) for n in range(PIECES)]
    even, uneven = odd == 0, odd == 1
    count = [0]
    copies = []

    def remote(name, src, dst, to):
        n = count[0]
        count[0] += 1
        copy = pltpu.make_async_remote_copy(
            src_ref=src, dst_ref=dst, send_sem=send_sem.at[n], recv_sem=recv_sem.at[n],
            device_id={name: to}, device_id_type=MESH,
        )
        copies.append(copy)
        return copy

    def send(name, src, dst, to):
        copy = remote(name, src, dst, to)
        copy.start()
        return copy

    def send_all(name, source, landing):
        return [send(name, source(d), landing(d - 1), peer(name, d)) for d in range(1, size[name])]

    def start(group):
        for copy in group:
            copy.start()

    def arrived(group):
        for copy in group:
            copy.wait_recv()

    def total_of(first, rest):
        for one in rest:
            first = first + one
        return first

    def hand_over(h):
        there = gathered_ref.at[me["bz"], h]
        return send_all("bz", lambda d: there, lambda n: there)

    class Tree:
        def start(self):
            share = half // nz
            mine = pl.ds(me["bz"] * share, share)
            self.rows_there = core_rows_ref.at[mine, :, pl.ds(ni, ni)]
            self.rows_sent = send("bx", core_rows_hbm.at[mine, 1 - odd], self.rows_there, partner)
            self.paired_sent, self.part_sent, self.full = [[] for _ in range(chunks)], [], []

        def load(self):
            self.own_rows = [load(core_rows_hbm.at[:, odd], core_rows_ref.at[:, :, pl.ds(0, ni)])]

        def reduced(self, h, piece, total):
            held[h, 0, piece] = total
            self.paired_sent[h].append(send("bx", held.at[h, 0, piece], held.at[h, 1, piece], partner))

        def share(self):
            arrived([self.rows_sent])
            self.rows_shared = send_all("bz", lambda d: self.rows_there, lambda n: self.rows_there)

        def forward(self, h):
            pass

        def combine(self, h):
            if h == 0:
                ready(self.own_rows)
                arrived(self.rows_shared)
            arrived(self.paired_sent[h])
            data = split(held[h].reshape(2 * ni, wide))
            group = []
            for d in range(1, half + 1):
                to = lax.rem(pair + d, half)
                part[d - 1, h] = dot3(split(core_rows_ref[to]), data, NN)
                if d < half:
                    group.append(remote("bx", part.at[d - 1, h], part_in.at[d - 1, h], 2 * to + odd))
            self.part_sent.append(group)
            start(group)

        def finish(self, h):
            arrived(self.part_sent[h])
            gathered_ref[me["bz"], h] = total_of(part[half - 1, h], [part_in[d, h] for d in range(half - 1)])
            self.full += hand_over(h)

    core = Tree()
    core.load()
    col_test_load = [load(col_test_hbm, col_test_ref)]
    planes_load = [load(core_planes_hbm, core_planes_ref)]

    ready(slab_load)
    slab = split(slab_ref[0])
    shrunk_sent = []

    def shrink(h):
        ready(cols_load[h])
        terms = dot3(slab, split(core_cols_ref[h]), NT)
        for y in range(ny):
            shrunk[y, h] = terms[:, y * wide:(y + 1) * wide]

    def send_shrunk(h):
        shrunk_sent.append([
            send_all("by", lambda d: shrunk.at[peer("by", d), h, piece], lambda n: shrunk_in.at[n, h, piece])
            for piece in pieces
        ])

    shrink(0)
    pl.semaphore_wait(barrier, nx + ny + nz - 3)
    send_shrunk(0)
    core.start()

    ready(first_load)
    row_test = row_test_ref[...]
    plane_test = plane_test_ref[...]
    scaled = split((row_test * plane_test).T)
    terms = dot3(scaled, slab, NN)
    block = col_a.shape[3]
    for x in range(nx):
        for z in range(nz):
            first = (x * nz + z) * block
            col_a[z, x // 2, x % 2] = terms[first:first + block, :]
    col_a_sent = send_all("bz", lambda d: col_a.at[peer("bz", d)], lambda n: col_a_in.at[n])

    for h in range(1, chunks):
        shrink(h)
        send_shrunk(h)

    def reduce_shrunk(h):
        for piece, group in zip(pieces, shrunk_sent[h]):
            arrived(group)
            total = total_of(shrunk[me["by"], h, piece], [shrunk_in[d, h, piece] for d in range(ny - 1)])
            core.reduced(h, piece, total)

    arrived(col_a_sent)
    col_b[...] = total_of(col_a[me["bz"]], [col_a_in[d] for d in range(nz - 1)])

    col_b_sent = []
    for d in range(1, half):
        to = lax.rem(pair + d, half)
        col_b_sent.append(send("bx", col_b.at[to, 0], col_b_in.at[d - 1], 2 * to + odd))

    reduce_shrunk(0)

    ready(planes_load)
    for p in range(core_planes_ref.shape[0]):
        line = core_planes_ref[p:p + 1, :]
        planes_ref[p] = jnp.broadcast_to(line, (128, line.shape[1])).T

    for h in range(1, chunks):
        reduce_shrunk(h)

    core.share()
    near_sent = remote("bx", col_b.at[:, 1], col_near_in, partner)
    pl.when(even)(lambda: start([near_sent]))


    ready(col_test_load)
    by_col = dot3(slab, split(col_test_ref[...]), NN)
    plane_a[...] = jnp.sum(by_col * row_test, axis=0, keepdims=True)
    plane_a_sent = send_all("by", lambda d: plane_a, lambda n: plane_a_in.at[n])
    terms = (by_col * plane_test).T
    block = row_a.shape[2]
    for y in range(ny):
        for z in range(nz):
            first = (y * nz + z) * block
            row_a[z, y] = terms[first:first + block, :]
    row_a_sent = send_all("bz", lambda d: row_a.at[peer("bz", d)], lambda n: row_a_in.at[n])

    for h in range(chunks):
        core.forward(h)

    arrived(plane_a_sent)
    plane_b[...] = total_of(plane_a[...], [plane_a_in[d] for d in range(ny - 1)])
    plane_b_sent = send_all("bx", lambda d: plane_b, lambda n: plane_b_in.at[n])

    arrived(row_a_sent)
    row_b[...] = total_of(row_a[me["bz"]], [row_a_in[d] for d in range(nz - 1)])
    row_b_sent = send_all("by", lambda d: row_b.at[peer("by", d)], lambda n: row_b_in.at[n])

    core.combine(0)

    for h in range(1, chunks):
        core.combine(h)

    arrived(col_b_sent)
    col_c[...] = total_of(col_b[pair, 0], [col_b_in[d] for d in range(half - 1)])
    home_sent = remote("bx", col_c, col_c_in, partner)
    pl.when(uneven)(lambda: start([home_sent]))

    far_sent = [
        remote("bx", col_near.at[lax.rem(pair + d, half)], col_far_in.at[d - 1], 2 * lax.rem(pair + d, half) + odd)
        for d in range(1, half)
    ]

    @pl.when(uneven)
    def _():
        near_sent.wait_recv()
        col_near[...] = col_b[:, 1] + col_near_in[...]
        start(far_sent)

    arrived(row_b_sent)
    row_ref[...] = total_of(row_b[me["by"]], [row_b_in[d] for d in range(ny - 1)])

    arrived(plane_b_sent)
    plane_ref[...] = total_of(plane_b[...], [plane_b_in[d] for d in range(nx - 1)])

    for h in range(chunks):
        core.finish(h)

    @pl.when(even)
    def _():
        home_sent.wait_recv()
        col_ref[...] = col_c[...] + col_c_in[...]
        near_sent.wait_send()

    @pl.when(uneven)
    def _():
        arrived(far_sent)
        col_ref[...] = total_of(col_near[pair], [col_far_in[d] for d in range(half - 1)])
        for copy in [home_sent] + far_sent:
            copy.wait_send()

    arrived(core.full)
    for copy in copies:
        if all(copy is not one for one in [near_sent, home_sent] + far_sent):
            copy.wait_send()


def core_kernel(
    planes_ref, gathered_ref, row_in, col_in, plane_in,
    row_ref, col_ref, plane_ref, out_ref,
    slots, out_sem, small_sem,
):
    count, rows = slots.shape[:2]
    steps = out_ref.shape[0] // rows
    planes, chunks, _, wide = gathered_ref.shape
    small = [
        pltpu.make_async_copy(source, target, small_sem.at[n])
        for n, (source, target) in enumerate(((row_in, row_ref), (col_in, col_ref), (plane_in, plane_ref)))
    ]

    def copy(step, slot):
        return pltpu.make_async_copy(
            slots.at[slot], out_ref.at[pl.ds(step * rows, rows)], out_sem.at[slot]
        )

    def body(step, _):
        slot = lax.rem(step, count)

        @pl.when(step >= count)
        def _():
            copy(step - count, slot).wait()

        for c in range(rows):
            row = step * rows + c
            value = [planes_ref[p, pl.ds(row, 1), :] for p in range(planes)]
            for h in range(chunks):
                total = value[0] * gathered_ref[0, h]
                for p in range(1, planes):
                    total = total + value[p] * gathered_ref[p, h]
                slots[slot, c, :, h * wide:(h + 1) * wide] = total
        copy(step, slot).start()
        return 0

    lax.fori_loop(0, steps, body, 0)
    for one in small:
        one.start()
    for step in range(steps - count, steps):
        copy(step, step % count).wait()
    for one in small:
        one.wait()


def on_device(nx, ny, nz, slab, plane_test, row_test, col_test, core_planes, core_rows, core_cols):
    rank = row_test.shape[1]
    ni, nj = slab.shape[1:]
    ab, bb = core_rows.shape[0] // nx, core_cols.shape[0] // ny
    rb, cb = rank // (ny * nz), rank // (nx * nz)
    half = nx // 2
    wide = 128
    chunks = bb // wide
    depth, planes = core_planes.shape
    shape = lambda *dims: jax.ShapeDtypeStruct(dims, F32)
    vmem = lambda *dims: pltpu.VMEM(dims, F32)
    inputs = (
        slab, plane_test, row_test, col_test, core_planes.T,
        core_rows.reshape(half, 2, ab, ni), core_cols,
    )
    transfers = 4 * (nz + ny + nx) + chunks * (nz + 2 * PIECES * ny + half + 4)
    gathered, row_t, plane_sketch, planes_wide, col_t = pl.pallas_call(
        functools.partial(exchange_kernel, nx, ny, nz),
        out_shape=(
            shape(nz, chunks, ab, wide), shape(rb, ni), shape(1, rank), shape(planes, depth, 128),
            shape(cb, nj),
        ),
        in_specs=[pl.BlockSpec(memory_space=pltpu.HBM)] * 7,
        out_specs=[pl.BlockSpec(memory_space=pltpu.VMEM)] * 5,
        scratch_shapes=[
            vmem(1, ni, nj), vmem(1, rank), vmem(ni, rank), vmem(nj, rank), vmem(planes, depth),
            vmem(half, ab, 2 * ni), vmem(chunks, ny * wide, nj),
            vmem(ny, chunks, ni, wide), vmem(ny - 1, chunks, ni, wide),
            vmem(chunks, 2, ni, wide),
            vmem(half, chunks, ab, wide), vmem(half - 1, chunks, ab, wide),
            vmem(nz, ny, rb, ni), vmem(nz - 1, ny, rb, ni),
            vmem(ny, rb, ni), vmem(ny - 1, rb, ni),
            vmem(nz, half, 2, cb, nj), vmem(nz - 1, half, 2, cb, nj),
            vmem(half, 2, cb, nj), vmem(half - 1, cb, nj), vmem(cb, nj), vmem(cb, nj),
            vmem(half, cb, nj), vmem(half, cb, nj), vmem(half - 1, cb, nj),
            vmem(1, rank), vmem(ny - 1, 1, rank),
            vmem(1, rank), vmem(nx - 1, 1, rank),
            pltpu.SemaphoreType.DMA((transfers,)),
            pltpu.SemaphoreType.DMA((transfers,)),
            pltpu.SemaphoreType.DMA((7 + chunks * ny,)),
        ],
        compiler_params=pltpu.CompilerParams(
            collective_id=0, has_side_effects=True, vmem_limit_bytes=32 << 20
        ),
        name="exchange",
    )(*(pltpu.with_memory_space_constraint(a, pltpu.HBM) for a in inputs))
    rows = min(depth, max(1, (1 << 17) // (ab * bb)))
    slots = min(8, depth // rows)
    row_t, col_t, plane_sketch, core_sketch = pl.pallas_call(
        core_kernel,
        out_shape=(shape(rb, ni), shape(cb, nj), shape(1, rank), shape(depth, ab, bb)),
        in_specs=[pl.BlockSpec(memory_space=pltpu.VMEM)] * 5,
        out_specs=[pl.BlockSpec(memory_space=pltpu.HBM)] * 4,
        scratch_shapes=[
            vmem(slots, rows, ab, bb),
            pltpu.SemaphoreType.DMA((slots,)),
            pltpu.SemaphoreType.DMA((3,)),
        ],
        compiler_params=pltpu.CompilerParams(vmem_limit_bytes=16 << 20),
        cost_estimate=pl.CostEstimate(flops=3 * depth * ab * bb, bytes_accessed=4 * depth * ab * bb, transcendentals=0),
        name="core",
    )(planes_wide, gathered, row_t, col_t, plane_sketch)
    return plane_sketch, row_t.T, col_t.T, core_sketch


def solution(mesh):
    in_specs = (
        P(("groups", "bz"), "bx", "by"),
        P("bz", None),
        P("bx", None),
        P("by", None),
        P("bz", None),
        P(None, "bx"),
        P(None, "by"),
    )
    out_specs = (
        P(("groups", "bz"), None),
        P(("groups", "bx"), ("by", "bz")),
        P(("groups", "by"), ("bx", "bz")),
        P(("groups", "bz"), "bx", "by"),
    )
    sizes = [mesh.shape[name] for name in ("bx", "by", "bz")]
    return jax.shard_map(
        functools.partial(on_device, *sizes),
        mesh=mesh, in_specs=in_specs, out_specs=out_specs, check_vma=False,
    )
```

```python
import functools

import jax
import jax.numpy as jnp
from jax import lax
from jax.experimental import pallas as pl
from jax.experimental.pallas import tpu as pltpu
from jax.sharding import PartitionSpec as P

F32 = jnp.float32
MESH = pl.DeviceIdType.MESH


def split(x):
    high = x.astype(jnp.bfloat16)
    return high, (x - high.astype(F32)).astype(jnp.bfloat16)


def dot3(a, b, dims):
    f = functools.partial(
        lax.dot_general, dimension_numbers=(dims, ((), ())), preferred_element_type=F32
    )
    return f(a[0], b[0]) + (f(a[0], b[1]) + f(a[1], b[0]))


NN = ((1,), (0,))
NT = ((1,), (1,))


PIECES = 1


def exchange_kernel(
    nx, ny, nz,
    slab_hbm, plane_test_hbm, row_test_hbm, col_test_hbm, core_planes_hbm, core_rows_hbm, core_cols_hbm,
    gathered_ref, row_ref, plane_ref, planes_ref, col_ref,
    slab_ref, plane_test_ref, row_test_ref, col_test_ref, core_planes_ref, core_rows_ref, core_cols_ref,
    shrunk, shrunk_in, held, part, part_in,
    row_a, row_a_in, row_b, row_b_in,
    col_a, col_a_in, col_b, col_b_in, col_c, col_c_in, col_near, col_near_in, col_far_in,
    plane_a, plane_a_in, plane_b, plane_b_in,
    send_sem, recv_sem, load_sem,
):
    size = {"bx": nx, "by": ny, "bz": nz}
    me = {name: lax.axis_index(name) for name in size}
    odd, pair = lax.rem(me["bx"], 2), lax.div(me["bx"], 2)
    half = nx // 2
    partner = 2 * pair + 1 - odd
    chunks, ni, wide = shrunk.shape[1:]

    loads = []

    def load(source, target):
        copy = pltpu.make_async_copy(source, target, load_sem.at[len(loads)])
        copy.start()
        loads.append(copy)
        return copy

    def cols_of(h):
        return [
            load(core_cols_hbm.at[pl.ds((y * chunks + h) * wide, wide)], core_cols_ref.at[h, pl.ds(y * wide, wide)])
            for y in range(ny)
        ]

    slab_load = [load(slab_hbm, slab_ref)]
    cols_load = [cols_of(0)]
    first_load = [load(row_test_hbm, row_test_ref), load(plane_test_hbm, plane_test_ref)]
    cols_load += [cols_of(h) for h in range(1, chunks)]

    def ready(group):
        for copy in group:
            copy.wait()

    def peer(name, d):
        return lax.rem(me[name] + d, size[name])

    barrier = pltpu.get_barrier_semaphore()
    for name in size:
        for d in range(1, size[name]):
            pl.semaphore_signal(barrier, inc=1, device_id={name: peer(name, d)}, device_id_type=MESH)

    pieces = [pl.ds(n * ni // PIECES, ni // PIECES) for n in range(PIECES)]
    even, uneven = odd == 0, odd == 1
    count = [0]
    copies = []

    def remote(name, src, dst, to):
        n = count[0]
        count[0] += 1
        copy = pltpu.make_async_remote_copy(
            src_ref=src, dst_ref=dst, send_sem=send_sem.at[n], recv_sem=recv_sem.at[n],
            device_id={name: to}, device_id_type=MESH,
        )
        copies.append(copy)
        return copy

    def send(name, src, dst, to):
        copy = remote(name, src, dst, to)
        copy.start()
        return copy

    def send_all(name, source, landing):
        return [send(name, source(d), landing(d - 1), peer(name, d)) for d in range(1, size[name])]

    def start(group):
        for copy in group:
            copy.start()

    def arrived(group):
        for copy in group:
            copy.wait_recv()

    def total_of(first, rest):
        for one in rest:
            first = first + one
        return first

    def hand_over(h):
        there = gathered_ref.at[me["bz"], h]
        return send_all("bz", lambda d: there, lambda n: there)

    class Tree:
        def start(self):
            share = half // nz
            mine = pl.ds(me["bz"] * share, share)
            self.rows_there = core_rows_ref.at[mine, :, pl.ds(ni, ni)]
            self.rows_sent = send("bx", core_rows_hbm.at[mine, 1 - odd], self.rows_there, partner)
            self.paired_sent, self.part_sent, self.full = [[] for _ in range(chunks)], [], []

        def load(self):
            self.own_rows = [load(core_rows_hbm.at[:, odd], core_rows_ref.at[:, :, pl.ds(0, ni)])]

        def reduced(self, h, piece, total):
            held[h, 0, piece] = total
            self.paired_sent[h].append(send("bx", held.at[h, 0, piece], held.at[h, 1, piece], partner))

        def share(self):
            arrived([self.rows_sent])
            self.rows_shared = send_all("bz", lambda d: self.rows_there, lambda n: self.rows_there)

        def forward(self, h):
            pass

        def combine(self, h):
            if h == 0:
                ready(self.own_rows)
                arrived(self.rows_shared)
            arrived(self.paired_sent[h])
            data = split(held[h].reshape(2 * ni, wide))
            group = []
            for d in range(1, half + 1):
                to = lax.rem(pair + d, half)
                part[d - 1, h] = dot3(split(core_rows_ref[to]), data, NN)
                if d < half:
                    group.append(remote("bx", part.at[d - 1, h], part_in.at[d - 1, h], 2 * to + odd))
            self.part_sent.append(group)
            start(group)

        def finish(self, h):
            arrived(self.part_sent[h])
            gathered_ref[me["bz"], h] = total_of(part[half - 1, h], [part_in[d, h] for d in range(half - 1)])
            self.full += hand_over(h)

    core = Tree()
    core.load()
    col_test_load = [load(col_test_hbm, col_test_ref)]
    planes_load = [load(core_planes_hbm, core_planes_ref)]

    ready(slab_load)
    slab = split(slab_ref[0])
    shrunk_sent = []

    def shrink(h):
        ready(cols_load[h])
        terms = dot3(slab, split(core_cols_ref[h]), NT)
        for y in range(ny):
            shrunk[y, h] = terms[:, y * wide:(y + 1) * wide]

    def send_shrunk(h):
        shrunk_sent.append([
            send_all("by", lambda d: shrunk.at[peer("by", d), h, piece], lambda n: shrunk_in.at[n, h, piece])
            for piece in pieces
        ])

    shrink(0)
    pl.semaphore_wait(barrier, nx + ny + nz - 3)
    send_shrunk(0)
    core.start()

    for h in range(1, chunks):
        shrink(h)
        send_shrunk(h)

    ready(first_load)
    row_test = row_test_ref[...]
    plane_test = plane_test_ref[...]
    scaled = split((row_test * plane_test).T)
    terms = dot3(scaled, slab, NN)
    block = col_a.shape[3]
    for x in range(nx):
        for z in range(nz):
            first = (x * nz + z) * block
            col_a[z, x // 2, x % 2] = terms[first:first + block, :]
    col_a_sent = send_all("bz", lambda d: col_a.at[peer("bz", d)], lambda n: col_a_in.at[n])

    def reduce_shrunk(h):
        for piece, group in zip(pieces, shrunk_sent[h]):
            arrived(group)
            total = total_of(shrunk[me["by"], h, piece], [shrunk_in[d, h, piece] for d in range(ny - 1)])
            core.reduced(h, piece, total)

    arrived(col_a_sent)
    col_b[...] = total_of(col_a[me["bz"]], [col_a_in[d] for d in range(nz - 1)])

    col_b_sent = []
    for d in range(1, half):
        to = lax.rem(pair + d, half)
        col_b_sent.append(send("bx", col_b.at[to, 0], col_b_in.at[d - 1], 2 * to + odd))

    reduce_shrunk(0)

    ready(planes_load)
    for p in range(core_planes_ref.shape[0]):
        line = core_planes_ref[p:p + 1, :]
        planes_ref[p] = jnp.broadcast_to(line, (128, line.shape[1])).T

    for h in range(1, chunks):
        reduce_shrunk(h)

    core.share()
    near_sent = remote("bx", col_b.at[:, 1], col_near_in, partner)
    pl.when(even)(lambda: start([near_sent]))


    ready(col_test_load)
    by_col = dot3(slab, split(col_test_ref[...]), NN)
    plane_a[...] = jnp.sum(by_col * row_test, axis=0, keepdims=True)
    plane_a_sent = send_all("by", lambda d: plane_a, lambda n: plane_a_in.at[n])
    terms = (by_col * plane_test).T
    block = row_a.shape[2]
    for y in range(ny):
        for z in range(nz):
            first = (y * nz + z) * block
            row_a[z, y] = terms[first:first + block, :]
    row_a_sent = send_all("bz", lambda d: row_a.at[peer("bz", d)], lambda n: row_a_in.at[n])

    for h in range(chunks):
        core.forward(h)

    arrived(plane_a_sent)
    plane_b[...] = total_of(plane_a[...], [plane_a_in[d] for d in range(ny - 1)])
    plane_b_sent = send_all("bx", lambda d: plane_b, lambda n: plane_b_in.at[n])

    arrived(row_a_sent)
    row_b[...] = total_of(row_a[me["bz"]], [row_a_in[d] for d in range(nz - 1)])
    row_b_sent = send_all("by", lambda d: row_b.at[peer("by", d)], lambda n: row_b_in.at[n])

    core.combine(0)

    arrived(col_b_sent)
    col_c[...] = total_of(col_b[pair, 0], [col_b_in[d] for d in range(half - 1)])
    home_sent = remote("bx", col_c, col_c_in, partner)
    pl.when(uneven)(lambda: start([home_sent]))


    for h in range(1, chunks):
        core.combine(h)

    arrived(row_b_sent)
    row_ref[...] = total_of(row_b[me["by"]], [row_b_in[d] for d in range(ny - 1)])

    arrived(plane_b_sent)
    plane_ref[...] = total_of(plane_b[...], [plane_b_in[d] for d in range(nx - 1)])

    core.finish(0)

    far_sent = [
        remote("bx", col_near.at[lax.rem(pair + d, half)], col_far_in.at[d - 1], 2 * lax.rem(pair + d, half) + odd)
        for d in range(1, half)
    ]

    @pl.when(uneven)
    def _():
        near_sent.wait_recv()
        col_near[...] = col_b[:, 1] + col_near_in[...]
        start(far_sent)

    for h in range(1, chunks):
        core.finish(h)

    @pl.when(even)
    def _():
        home_sent.wait_recv()
        col_ref[...] = col_c[...] + col_c_in[...]
        near_sent.wait_send()

    @pl.when(uneven)
    def _():
        arrived(far_sent)
        col_ref[...] = total_of(col_near[pair], [col_far_in[d] for d in range(half - 1)])
        for copy in [home_sent] + far_sent:
            copy.wait_send()

    arrived(core.full)
    for copy in copies:
        if all(copy is not one for one in [near_sent, home_sent] + far_sent):
            copy.wait_send()


def core_kernel(
    planes_ref, gathered_ref, row_in, col_in, plane_in,
    row_ref, col_ref, plane_ref, out_ref,
    slots, out_sem, small_sem,
):
    count, rows = slots.shape[:2]
    steps = out_ref.shape[0] // rows
    planes, chunks, _, wide = gathered_ref.shape
    small = [
        pltpu.make_async_copy(source, target, small_sem.at[n])
        for n, (source, target) in enumerate(((row_in, row_ref), (col_in, col_ref), (plane_in, plane_ref)))
    ]

    def copy(step, slot):
        return pltpu.make_async_copy(
            slots.at[slot], out_ref.at[pl.ds(step * rows, rows)], out_sem.at[slot]
        )

    def body(step, _):
        slot = lax.rem(step, count)

        @pl.when(step >= count)
        def _():
            copy(step - count, slot).wait()

        for c in range(rows):
            row = step * rows + c
            value = [planes_ref[p, pl.ds(row, 1), :] for p in range(planes)]
            for h in range(chunks):
                total = value[0] * gathered_ref[0, h]
                for p in range(1, planes):
                    total = total + value[p] * gathered_ref[p, h]
                slots[slot, c, :, h * wide:(h + 1) * wide] = total
        copy(step, slot).start()
        return 0

    lax.fori_loop(0, steps, body, 0)
    for one in small:
        one.start()
    for step in range(steps - count, steps):
        copy(step, step % count).wait()
    for one in small:
        one.wait()


def on_device(nx, ny, nz, slab, plane_test, row_test, col_test, core_planes, core_rows, core_cols):
    rank = row_test.shape[1]
    ni, nj = slab.shape[1:]
    ab, bb = core_rows.shape[0] // nx, core_cols.shape[0] // ny
    rb, cb = rank // (ny * nz), rank // (nx * nz)
    half = nx // 2
    wide = 128
    chunks = bb // wide
    depth, planes = core_planes.shape
    shape = lambda *dims: jax.ShapeDtypeStruct(dims, F32)
    vmem = lambda *dims: pltpu.VMEM(dims, F32)
    inputs = (
        slab, plane_test, row_test, col_test, core_planes.T,
        core_rows.reshape(half, 2, ab, ni), core_cols,
    )
    transfers = 4 * (nz + ny + nx) + chunks * (nz + 2 * PIECES * ny + half + 4)
    gathered, row_t, plane_sketch, planes_wide, col_t = pl.pallas_call(
        functools.partial(exchange_kernel, nx, ny, nz),
        out_shape=(
            shape(nz, chunks, ab, wide), shape(rb, ni), shape(1, rank), shape(planes, depth, 128),
            shape(cb, nj),
        ),
        in_specs=[pl.BlockSpec(memory_space=pltpu.HBM)] * 7,
        out_specs=[pl.BlockSpec(memory_space=pltpu.VMEM)] * 5,
        scratch_shapes=[
            vmem(1, ni, nj), vmem(1, rank), vmem(ni, rank), vmem(nj, rank), vmem(planes, depth),
            vmem(half, ab, 2 * ni), vmem(chunks, ny * wide, nj),
            vmem(ny, chunks, ni, wide), vmem(ny - 1, chunks, ni, wide),
            vmem(chunks, 2, ni, wide),
            vmem(half, chunks, ab, wide), vmem(half - 1, chunks, ab, wide),
            vmem(nz, ny, rb, ni), vmem(nz - 1, ny, rb, ni),
            vmem(ny, rb, ni), vmem(ny - 1, rb, ni),
            vmem(nz, half, 2, cb, nj), vmem(nz - 1, half, 2, cb, nj),
            vmem(half, 2, cb, nj), vmem(half - 1, cb, nj), vmem(cb, nj), vmem(cb, nj),
            vmem(half, cb, nj), vmem(half, cb, nj), vmem(half - 1, cb, nj),
            vmem(1, rank), vmem(ny - 1, 1, rank),
            vmem(1, rank), vmem(nx - 1, 1, rank),
            pltpu.SemaphoreType.DMA((transfers,)),
            pltpu.SemaphoreType.DMA((transfers,)),
            pltpu.SemaphoreType.DMA((7 + chunks * ny,)),
        ],
        compiler_params=pltpu.CompilerParams(
            collective_id=0, has_side_effects=True, vmem_limit_bytes=32 << 20
        ),
        name="exchange",
    )(*(pltpu.with_memory_space_constraint(a, pltpu.HBM) for a in inputs))
    rows = min(depth, max(1, (1 << 17) // (ab * bb)))
    slots = min(8, depth // rows)
    row_t, col_t, plane_sketch, core_sketch = pl.pallas_call(
        core_kernel,
        out_shape=(shape(rb, ni), shape(cb, nj), shape(1, rank), shape(depth, ab, bb)),
        in_specs=[pl.BlockSpec(memory_space=pltpu.VMEM)] * 5,
        out_specs=[pl.BlockSpec(memory_space=pltpu.HBM)] * 4,
        scratch_shapes=[
            vmem(slots, rows, ab, bb),
            pltpu.SemaphoreType.DMA((slots,)),
            pltpu.SemaphoreType.DMA((3,)),
        ],
        compiler_params=pltpu.CompilerParams(vmem_limit_bytes=16 << 20),
        cost_estimate=pl.CostEstimate(flops=3 * depth * ab * bb, bytes_accessed=4 * depth * ab * bb, transcendentals=0),
        name="core",
    )(planes_wide, gathered, row_t, col_t, plane_sketch)
    return plane_sketch, row_t.T, col_t.T, core_sketch


def solution(mesh):
    in_specs = (
        P(("groups", "bz"), "bx", "by"),
        P("bz", None),
        P("bx", None),
        P("by", None),
        P("bz", None),
        P(None, "bx"),
        P(None, "by"),
    )
    out_specs = (
        P(("groups", "bz"), None),
        P(("groups", "bx"), ("by", "bz")),
        P(("groups", "by"), ("bx", "bz")),
        P(("groups", "bz"), "bx", "by"),
    )
    sizes = [mesh.shape[name] for name in ("bx", "by", "bz")]
    return jax.shard_map(
        functools.partial(on_device, *sizes),
        mesh=mesh, in_specs=in_specs, out_specs=out_specs, check_vma=False,
    )
```

```python
import functools

import jax
import jax.numpy as jnp
from jax import lax
from jax.experimental import pallas as pl
from jax.experimental.pallas import tpu as pltpu
from jax.sharding import PartitionSpec as P

F32 = jnp.float32
MESH = pl.DeviceIdType.MESH


def split(x):
    high = x.astype(jnp.bfloat16)
    return high, (x - high.astype(F32)).astype(jnp.bfloat16)


def dot3(a, b, dims):
    f = functools.partial(
        lax.dot_general, dimension_numbers=(dims, ((), ())), preferred_element_type=F32
    )
    return f(a[0], b[0]) + (f(a[0], b[1]) + f(a[1], b[0]))


NN = ((1,), (0,))
NT = ((1,), (1,))


PIECES = 1


def exchange_kernel(
    nx, ny, nz,
    slab_hbm, plane_test_hbm, row_test_hbm, col_test_hbm, core_planes_hbm, core_rows_hbm, core_cols_hbm,
    gathered_ref, row_ref, plane_ref, planes_ref, col_ref,
    slab_ref, plane_test_ref, row_test_ref, col_test_ref, core_planes_ref, core_rows_ref, core_cols_ref,
    shrunk, shrunk_in, held, part, part_in,
    row_a, row_a_in, row_b, row_b_in,
    col_a, col_a_in, col_b, col_b_in, col_c, col_c_in, col_near, col_near_in, col_far_in,
    plane_a, plane_a_in, plane_b, plane_b_in,
    send_sem, recv_sem, load_sem,
):
    size = {"bx": nx, "by": ny, "bz": nz}
    me = {name: lax.axis_index(name) for name in size}
    odd, pair = lax.rem(me["bx"], 2), lax.div(me["bx"], 2)
    half = nx // 2
    partner = 2 * pair + 1 - odd
    chunks, ni, wide = shrunk.shape[1:]

    loads = []

    def load(source, target):
        copy = pltpu.make_async_copy(source, target, load_sem.at[len(loads)])
        copy.start()
        loads.append(copy)
        return copy

    def cols_of(h):
        return [
            load(core_cols_hbm.at[pl.ds((y * chunks + h) * wide, wide)], core_cols_ref.at[h, pl.ds(y * wide, wide)])
            for y in range(ny)
        ]

    slab_load = [load(slab_hbm, slab_ref)]
    cols_load = [cols_of(0)]
    first_load = [load(row_test_hbm, row_test_ref), load(plane_test_hbm, plane_test_ref)]
    cols_load += [cols_of(h) for h in range(1, chunks)]

    def ready(group):
        for copy in group:
            copy.wait()

    def peer(name, d):
        return lax.rem(me[name] + d, size[name])

    barrier = pltpu.get_barrier_semaphore()
    for name in size:
        for d in range(1, size[name]):
            pl.semaphore_signal(barrier, inc=1, device_id={name: peer(name, d)}, device_id_type=MESH)

    pieces = [pl.ds(n * ni // PIECES, ni // PIECES) for n in range(PIECES)]
    even, uneven = odd == 0, odd == 1
    count = [0]
    copies = []

    def remote(name, src, dst, to):
        n = count[0]
        count[0] += 1
        copy = pltpu.make_async_remote_copy(
            src_ref=src, dst_ref=dst, send_sem=send_sem.at[n], recv_sem=recv_sem.at[n],
            device_id={name: to}, device_id_type=MESH,
        )
        copies.append(copy)
        return copy

    def send(name, src, dst, to):
        copy = remote(name, src, dst, to)
        copy.start()
        return copy

    def send_all(name, source, landing):
        return [send(name, source(d), landing(d - 1), peer(name, d)) for d in range(1, size[name])]

    def start(group):
        for copy in group:
            copy.start()

    def arrived(group):
        for copy in group:
            copy.wait_recv()

    def total_of(first, rest):
        for one in rest:
            first = first + one
        return first

    def hand_over(h):
        there = gathered_ref.at[me["bz"], h]
        return send_all("bz", lambda d: there, lambda n: there)

    class Tree:
        def start(self):
            share = half // nz
            mine = pl.ds(me["bz"] * share, share)
            self.rows_there = core_rows_ref.at[mine, :, pl.ds(ni, ni)]
            self.rows_sent = send("bx", core_rows_hbm.at[mine, 1 - odd], self.rows_there, partner)
            self.paired_sent, self.part_sent, self.full = [[] for _ in range(chunks)], [], []

        def load(self):
            self.own_rows = [load(core_rows_hbm.at[:, odd], core_rows_ref.at[:, :, pl.ds(0, ni)])]

        def reduced(self, h, piece, total):
            held[h, 0, piece] = total
            self.paired_sent[h].append(send("bx", held.at[h, 0, piece], held.at[h, 1, piece], partner))

        def share(self):
            arrived([self.rows_sent])
            self.rows_shared = send_all("bz", lambda d: self.rows_there, lambda n: self.rows_there)

        def forward(self, h):
            pass

        def combine(self, h):
            if h == 0:
                ready(self.own_rows)
                arrived(self.rows_shared)
            arrived(self.paired_sent[h])
            data = split(held[h].reshape(2 * ni, wide))
            group = []
            for d in range(1, half + 1):
                to = lax.rem(pair + d, half)
                part[d - 1, h] = dot3(split(core_rows_ref[to]), data, NN)
                if d < half:
                    group.append(remote("bx", part.at[d - 1, h], part_in.at[d - 1, h], 2 * to + odd))
            self.part_sent.append(group)
            start(group)

        def finish(self, h):
            arrived(self.part_sent[h])
            gathered_ref[me["bz"], h] = total_of(part[half - 1, h], [part_in[d, h] for d in range(half - 1)])
            self.full += hand_over(h)

    core = Tree()
    core.load()
    col_test_load = [load(col_test_hbm, col_test_ref)]
    planes_load = [load(core_planes_hbm, core_planes_ref)]

    ready(slab_load)
    slab = split(slab_ref[0])
    shrunk_sent = []

    def shrink(h):
        ready(cols_load[h])
        terms = dot3(slab, split(core_cols_ref[h]), NT)
        for y in range(ny):
            shrunk[y, h] = terms[:, y * wide:(y + 1) * wide]

    def send_shrunk(h):
        shrunk_sent.append([
            send_all("by", lambda d: shrunk.at[peer("by", d), h, piece], lambda n: shrunk_in.at[n, h, piece])
            for piece in pieces
        ])

    shrink(0)
    pl.semaphore_wait(barrier, nx + ny + nz - 3)
    send_shrunk(0)
    core.start()

    for h in range(1, chunks):
        shrink(h)
        send_shrunk(h)

    ready(first_load)
    row_test = row_test_ref[...]
    plane_test = plane_test_ref[...]
    scaled = split((row_test * plane_test).T)
    terms = dot3(scaled, slab, NN)
    block = col_a.shape[3]
    for x in range(nx):
        for z in range(nz):
            first = (x * nz + z) * block
            col_a[z, x // 2, x % 2] = terms[first:first + block, :]
    col_a_sent = send_all("bz", lambda d: col_a.at[peer("bz", d)], lambda n: col_a_in.at[n])

    def reduce_shrunk(h):
        for piece, group in zip(pieces, shrunk_sent[h]):
            arrived(group)
            total = total_of(shrunk[me["by"], h, piece], [shrunk_in[d, h, piece] for d in range(ny - 1)])
            core.reduced(h, piece, total)

    arrived(col_a_sent)
    col_b[...] = total_of(col_a[me["bz"]], [col_a_in[d] for d in range(nz - 1)])

    col_b_sent = []
    for d in range(1, half):
        to = lax.rem(pair + d, half)
        col_b_sent.append(send("bx", col_b.at[to, 0], col_b_in.at[d - 1], 2 * to + odd))

    reduce_shrunk(0)

    ready(planes_load)
    for p in range(core_planes_ref.shape[0]):
        line = core_planes_ref[p:p + 1, :]
        planes_ref[p] = jnp.broadcast_to(line, (128, line.shape[1])).T

    for h in range(1, chunks):
        reduce_shrunk(h)

    core.share()
    near_sent = [
        remote("bx", col_b.at[to, 1], col_near_in.at[to], partner)
        for to in [lax.rem(pair + d, half) for d in range(1, half + 1)]
    ]
    pl.when(even)(lambda: start(near_sent))


    ready(col_test_load)
    by_col = dot3(slab, split(col_test_ref[...]), NN)
    plane_a[...] = jnp.sum(by_col * row_test, axis=0, keepdims=True)
    plane_a_sent = send_all("by", lambda d: plane_a, lambda n: plane_a_in.at[n])
    terms = (by_col * plane_test).T
    block = row_a.shape[2]
    for y in range(ny):
        for z in range(nz):
            first = (y * nz + z) * block
            row_a[z, y] = terms[first:first + block, :]
    row_a_sent = send_all("bz", lambda d: row_a.at[peer("bz", d)], lambda n: row_a_in.at[n])

    for h in range(chunks):
        core.forward(h)

    arrived(plane_a_sent)
    plane_b[...] = total_of(plane_a[...], [plane_a_in[d] for d in range(ny - 1)])
    plane_b_sent = send_all("bx", lambda d: plane_b, lambda n: plane_b_in.at[n])

    arrived(row_a_sent)
    row_b[...] = total_of(row_a[me["bz"]], [row_a_in[d] for d in range(nz - 1)])
    row_b_sent = send_all("by", lambda d: row_b.at[peer("by", d)], lambda n: row_b_in.at[n])

    core.combine(0)

    arrived(col_b_sent)
    col_c[...] = total_of(col_b[pair, 0], [col_b_in[d] for d in range(half - 1)])
    home_sent = remote("bx", col_c, col_c_in, partner)
    pl.when(uneven)(lambda: start([home_sent]))


    for h in range(1, chunks):
        core.combine(h)

    arrived(row_b_sent)
    row_ref[...] = total_of(row_b[me["by"]], [row_b_in[d] for d in range(ny - 1)])

    arrived(plane_b_sent)
    plane_ref[...] = total_of(plane_b[...], [plane_b_in[d] for d in range(nx - 1)])

    core.finish(0)

    far_sent = [
        remote("bx", col_near.at[lax.rem(pair + d, half)], col_far_in.at[d - 1], 2 * lax.rem(pair + d, half) + odd)
        for d in range(1, half)
    ]

    @pl.when(uneven)
    def _():
        for d in range(1, half + 1):
            to = lax.rem(pair + d, half)
            near_sent[d - 1].wait_recv()
            col_near[to] = col_b[to, 1] + col_near_in[to]
            if d < half:
                far_sent[d - 1].start()

    for h in range(1, chunks):
        core.finish(h)

    @pl.when(even)
    def _():
        home_sent.wait_recv()
        col_ref[...] = col_c[...] + col_c_in[...]
        for copy in near_sent:
            copy.wait_send()

    @pl.when(uneven)
    def _():
        arrived(far_sent)
        col_ref[...] = total_of(col_near[pair], [col_far_in[d] for d in range(half - 1)])
        for copy in [home_sent] + far_sent:
            copy.wait_send()

    arrived(core.full)
    for copy in copies:
        if all(copy is not one for one in near_sent + [home_sent] + far_sent):
            copy.wait_send()


def core_kernel(
    planes_ref, gathered_ref, row_in, col_in, plane_in,
    row_ref, col_ref, plane_ref, out_ref,
    slots, out_sem, small_sem,
):
    count, rows = slots.shape[:2]
    steps = out_ref.shape[0] // rows
    planes, chunks, _, wide = gathered_ref.shape
    small = [
        pltpu.make_async_copy(source, target, small_sem.at[n])
        for n, (source, target) in enumerate(((row_in, row_ref), (col_in, col_ref), (plane_in, plane_ref)))
    ]

    def copy(step, slot):
        return pltpu.make_async_copy(
            slots.at[slot], out_ref.at[pl.ds(step * rows, rows)], out_sem.at[slot]
        )

    def body(step, _):
        slot = lax.rem(step, count)

        @pl.when(step >= count)
        def _():
            copy(step - count, slot).wait()

        for c in range(rows):
            row = step * rows + c
            value = [planes_ref[p, pl.ds(row, 1), :] for p in range(planes)]
            for h in range(chunks):
                total = value[0] * gathered_ref[0, h]
                for p in range(1, planes):
                    total = total + value[p] * gathered_ref[p, h]
                slots[slot, c, :, h * wide:(h + 1) * wide] = total
        copy(step, slot).start()
        return 0

    for one in small:
        one.start()
    lax.fori_loop(0, steps, body, 0)
    for step in range(steps - count, steps):
        copy(step, step % count).wait()
    for one in small:
        one.wait()


def on_device(nx, ny, nz, slab, plane_test, row_test, col_test, core_planes, core_rows, core_cols):
    rank = row_test.shape[1]
    ni, nj = slab.shape[1:]
    ab, bb = core_rows.shape[0] // nx, core_cols.shape[0] // ny
    rb, cb = rank // (ny * nz), rank // (nx * nz)
    half = nx // 2
    wide = 128
    chunks = bb // wide
    depth, planes = core_planes.shape
    shape = lambda *dims: jax.ShapeDtypeStruct(dims, F32)
    vmem = lambda *dims: pltpu.VMEM(dims, F32)
    inputs = (
        slab, plane_test, row_test, col_test, core_planes.T,
        core_rows.reshape(half, 2, ab, ni), core_cols,
    )
    transfers = half + 4 * (nz + ny + nx) + chunks * (nz + 2 * PIECES * ny + half + 4)
    gathered, row_t, plane_sketch, planes_wide, col_t = pl.pallas_call(
        functools.partial(exchange_kernel, nx, ny, nz),
        out_shape=(
            shape(nz, chunks, ab, wide), shape(rb, ni), shape(1, rank), shape(planes, depth, 128),
            shape(cb, nj),
        ),
        in_specs=[pl.BlockSpec(memory_space=pltpu.HBM)] * 7,
        out_specs=[pl.BlockSpec(memory_space=pltpu.VMEM)] * 5,
        scratch_shapes=[
            vmem(1, ni, nj), vmem(1, rank), vmem(ni, rank), vmem(nj, rank), vmem(planes, depth),
            vmem(half, ab, 2 * ni), vmem(chunks, ny * wide, nj),
            vmem(ny, chunks, ni, wide), vmem(ny - 1, chunks, ni, wide),
            vmem(chunks, 2, ni, wide),
            vmem(half, chunks, ab, wide), vmem(half - 1, chunks, ab, wide),
            vmem(nz, ny, rb, ni), vmem(nz - 1, ny, rb, ni),
            vmem(ny, rb, ni), vmem(ny - 1, rb, ni),
            vmem(nz, half, 2, cb, nj), vmem(nz - 1, half, 2, cb, nj),
            vmem(half, 2, cb, nj), vmem(half - 1, cb, nj), vmem(cb, nj), vmem(cb, nj),
            vmem(half, cb, nj), vmem(half, cb, nj), vmem(half - 1, cb, nj),
            vmem(1, rank), vmem(ny - 1, 1, rank),
            vmem(1, rank), vmem(nx - 1, 1, rank),
            pltpu.SemaphoreType.DMA((transfers,)),
            pltpu.SemaphoreType.DMA((transfers,)),
            pltpu.SemaphoreType.DMA((7 + chunks * ny,)),
        ],
        compiler_params=pltpu.CompilerParams(
            collective_id=0, has_side_effects=True, vmem_limit_bytes=32 << 20
        ),
        name="exchange",
    )(*(pltpu.with_memory_space_constraint(a, pltpu.HBM) for a in inputs))
    rows = min(depth, max(1, (1 << 17) // (ab * bb)))
    slots = min(8, depth // rows)
    row_t, col_t, plane_sketch, core_sketch = pl.pallas_call(
        core_kernel,
        out_shape=(shape(rb, ni), shape(cb, nj), shape(1, rank), shape(depth, ab, bb)),
        in_specs=[pl.BlockSpec(memory_space=pltpu.VMEM)] * 5,
        out_specs=[pl.BlockSpec(memory_space=pltpu.HBM)] * 4,
        scratch_shapes=[
            vmem(slots, rows, ab, bb),
            pltpu.SemaphoreType.DMA((slots,)),
            pltpu.SemaphoreType.DMA((3,)),
        ],
        compiler_params=pltpu.CompilerParams(vmem_limit_bytes=16 << 20),
        cost_estimate=pl.CostEstimate(flops=3 * depth * ab * bb, bytes_accessed=4 * depth * ab * bb, transcendentals=0),
        name="core",
    )(planes_wide, gathered, row_t, col_t, plane_sketch)
    return plane_sketch, row_t.T, col_t.T, core_sketch


def solution(mesh):
    in_specs = (
        P(("groups", "bz"), "bx", "by"),
        P("bz", None),
        P("bx", None),
        P("by", None),
        P("bz", None),
        P(None, "bx"),
        P(None, "by"),
    )
    out_specs = (
        P(("groups", "bz"), None),
        P(("groups", "bx"), ("by", "bz")),
        P(("groups", "by"), ("bx", "bz")),
        P(("groups", "bz"), "bx", "by"),
    )
    sizes = [mesh.shape[name] for name in ("bx", "by", "bz")]
    return jax.shard_map(
        functools.partial(on_device, *sizes),
        mesh=mesh, in_specs=in_specs, out_specs=out_specs, check_vma=False,
    )
```

```python
import functools

import jax
import jax.numpy as jnp
from jax import lax
from jax.experimental import pallas as pl
from jax.experimental.pallas import tpu as pltpu
from jax.sharding import PartitionSpec as P

F32 = jnp.float32
MESH = pl.DeviceIdType.MESH


def split(x):
    high = x.astype(jnp.bfloat16)
    return high, (x - high.astype(F32)).astype(jnp.bfloat16)


def dot3(a, b, dims):
    f = functools.partial(
        lax.dot_general, dimension_numbers=(dims, ((), ())), preferred_element_type=F32
    )
    return f(a[0], b[0]) + (f(a[0], b[1]) + f(a[1], b[0]))


NN = ((1,), (0,))
NT = ((1,), (1,))


PIECES = 1


def exchange_kernel(
    nx, ny, nz,
    slab_hbm, plane_test_hbm, row_test_hbm, col_test_hbm, core_planes_hbm, core_rows_hbm, core_cols_hbm,
    gathered_ref, row_ref, plane_ref, planes_ref, col_ref,
    slab_ref, plane_test_ref, row_test_ref, col_test_ref, core_planes_ref, core_rows_ref, core_cols_ref,
    shrunk, shrunk_in, held, part, part_in,
    row_a, row_a_in, row_b, row_b_in,
    col_a, col_a_in, col_b, col_b_in, col_c, col_c_in, col_near, col_near_in, col_far_in,
    plane_a, plane_a_in, plane_b, plane_b_in,
    send_sem, recv_sem, load_sem,
):
    size = {"bx": nx, "by": ny, "bz": nz}
    me = {name: lax.axis_index(name) for name in size}
    odd, pair = lax.rem(me["bx"], 2), lax.div(me["bx"], 2)
    half = nx // 2
    partner = 2 * pair + 1 - odd
    chunks, ni, wide = shrunk.shape[1:]

    loads = []

    def load(source, target):
        copy = pltpu.make_async_copy(source, target, load_sem.at[len(loads)])
        copy.start()
        loads.append(copy)
        return copy

    def cols_of(h):
        return [
            load(core_cols_hbm.at[pl.ds((y * chunks + h) * wide, wide)], core_cols_ref.at[h, pl.ds(y * wide, wide)])
            for y in range(ny)
        ]

    slab_load = [load(slab_hbm, slab_ref)]
    cols_load = [cols_of(0)]
    first_load = [load(row_test_hbm, row_test_ref), load(plane_test_hbm, plane_test_ref)]
    cols_load += [cols_of(h) for h in range(1, chunks)]

    def ready(group):
        for copy in group:
            copy.wait()

    def peer(name, d):
        return lax.rem(me[name] + d, size[name])

    barrier = pltpu.get_barrier_semaphore()
    for name in size:
        for d in range(1, size[name]):
            pl.semaphore_signal(barrier, inc=1, device_id={name: peer(name, d)}, device_id_type=MESH)

    pieces = [pl.ds(n * ni // PIECES, ni // PIECES) for n in range(PIECES)]
    even, uneven = odd == 0, odd == 1
    count = [0]
    copies = []

    def remote(name, src, dst, to):
        n = count[0]
        count[0] += 1
        copy = pltpu.make_async_remote_copy(
            src_ref=src, dst_ref=dst, send_sem=send_sem.at[n], recv_sem=recv_sem.at[n],
            device_id={name: to}, device_id_type=MESH,
        )
        copies.append(copy)
        return copy

    def send(name, src, dst, to):
        copy = remote(name, src, dst, to)
        copy.start()
        return copy

    def send_all(name, source, landing):
        return [send(name, source(d), landing(d - 1), peer(name, d)) for d in range(1, size[name])]

    def start(group):
        for copy in group:
            copy.start()

    def arrived(group):
        for copy in group:
            copy.wait_recv()

    def total_of(first, rest):
        for one in rest:
            first = first + one
        return first

    def hand_over(h):
        there = gathered_ref.at[me["bz"], h]
        return send_all("bz", lambda d: there, lambda n: there)

    class Tree:
        def start(self):
            share = half // nz
            mine = pl.ds(me["bz"] * share, share)
            self.rows_there = core_rows_ref.at[mine, :, pl.ds(ni, ni)]
            self.rows_sent = send("bx", core_rows_hbm.at[mine, 1 - odd], self.rows_there, partner)
            self.paired_sent, self.part_sent, self.full = [[] for _ in range(chunks)], [], []

        def load(self):
            self.own_rows = [load(core_rows_hbm.at[:, odd], core_rows_ref.at[:, :, pl.ds(0, ni)])]

        def reduced(self, h, piece, total):
            held[h, 0, piece] = total
            self.paired_sent[h].append(send("bx", held.at[h, 0, piece], held.at[h, 1, piece], partner))

        def share(self):
            arrived([self.rows_sent])
            self.rows_shared = send_all("bz", lambda d: self.rows_there, lambda n: self.rows_there)

        def forward(self, h):
            pass

        def combine(self, h):
            if h == 0:
                ready(self.own_rows)
                arrived(self.rows_shared)
            arrived(self.paired_sent[h])
            data = split(held[h].reshape(2 * ni, wide))
            group = []
            for d in range(1, half + 1):
                to = lax.rem(pair + d, half)
                part[d - 1, h] = dot3(split(core_rows_ref[to]), data, NN)
                if d < half:
                    group.append(remote("bx", part.at[d - 1, h], part_in.at[d - 1, h], 2 * to + odd))
            self.part_sent.append(group)
            start(group)

        def finish(self, h):
            arrived(self.part_sent[h])
            gathered_ref[me["bz"], h] = total_of(part[half - 1, h], [part_in[d, h] for d in range(half - 1)])
            self.full += hand_over(h)

    core = Tree()
    core.load()
    col_test_load = [load(col_test_hbm, col_test_ref)]
    planes_load = [load(core_planes_hbm, core_planes_ref)]

    ready(slab_load)
    slab = split(slab_ref[0])
    shrunk_sent = []

    def shrink(h):
        ready(cols_load[h])
        terms = dot3(slab, split(core_cols_ref[h]), NT)
        for y in range(ny):
            shrunk[y, h] = terms[:, y * wide:(y + 1) * wide]

    def send_shrunk(h):
        shrunk_sent.append([
            send_all("by", lambda d: shrunk.at[peer("by", d), h, piece], lambda n: shrunk_in.at[n, h, piece])
            for piece in pieces
        ])

    shrink(0)
    pl.semaphore_wait(barrier, nx + ny + nz - 3)
    send_shrunk(0)
    core.start()

    for h in range(1, chunks):
        shrink(h)
        send_shrunk(h)

    ready(first_load)
    row_test = row_test_ref[...]
    plane_test = plane_test_ref[...]
    scaled = split((row_test * plane_test).T)
    terms = dot3(scaled, slab, NN)
    block = col_a.shape[3]
    for x in range(nx):
        for z in range(nz):
            first = (x * nz + z) * block
            col_a[z, x // 2, x % 2] = terms[first:first + block, :]
    col_a_sent = send_all("bz", lambda d: col_a.at[peer("bz", d)], lambda n: col_a_in.at[n])

    def reduce_shrunk(h):
        for piece, group in zip(pieces, shrunk_sent[h]):
            arrived(group)
            total = total_of(shrunk[me["by"], h, piece], [shrunk_in[d, h, piece] for d in range(ny - 1)])
            core.reduced(h, piece, total)

    arrived(col_a_sent)
    col_b[...] = total_of(col_a[me["bz"]], [col_a_in[d] for d in range(nz - 1)])

    col_b_sent = []
    for d in range(1, half):
        to = lax.rem(pair + d, half)
        col_b_sent.append(send("bx", col_b.at[to, 0], col_b_in.at[d - 1], 2 * to + odd))

    reduce_shrunk(0)

    ready(planes_load)
    for p in range(core_planes_ref.shape[0]):
        line = core_planes_ref[p:p + 1, :]
        planes_ref[p] = jnp.broadcast_to(line, (128, line.shape[1])).T

    for h in range(1, chunks):
        reduce_shrunk(h)

    core.share()
    near_sent = [
        remote("bx", col_b.at[to, 1], col_near_in.at[to], partner)
        for to in [lax.rem(pair + d, half) for d in range(1, half + 1)]
    ]
    pl.when(even)(lambda: start(near_sent))


    ready(col_test_load)
    by_col = dot3(slab, split(col_test_ref[...]), NN)
    plane_a[...] = jnp.sum(by_col * row_test, axis=0, keepdims=True)
    plane_a_sent = send_all("by", lambda d: plane_a, lambda n: plane_a_in.at[n])
    terms = (by_col * plane_test).T
    block = row_a.shape[2]
    for y in range(ny):
        for z in range(nz):
            first = (y * nz + z) * block
            row_a[z, y] = terms[first:first + block, :]
    row_a_sent = send_all("bz", lambda d: row_a.at[peer("bz", d)], lambda n: row_a_in.at[n])

    for h in range(chunks):
        core.forward(h)

    arrived(plane_a_sent)
    plane_b[...] = total_of(plane_a[...], [plane_a_in[d] for d in range(ny - 1)])
    plane_b_sent = send_all("bx", lambda d: plane_b, lambda n: plane_b_in.at[n])

    arrived(row_a_sent)
    row_b[...] = total_of(row_a[me["bz"]], [row_a_in[d] for d in range(nz - 1)])
    row_b_sent = send_all("by", lambda d: row_b.at[peer("by", d)], lambda n: row_b_in.at[n])

    core.combine(0)

    arrived(col_b_sent)
    col_c[...] = total_of(col_b[pair, 0], [col_b_in[d] for d in range(half - 1)])
    home_sent = remote("bx", col_c, col_c_in, partner)
    pl.when(uneven)(lambda: start([home_sent]))


    for h in range(1, chunks):
        core.combine(h)

    arrived(row_b_sent)
    row_ref[...] = total_of(row_b[me["by"]], [row_b_in[d] for d in range(ny - 1)])

    arrived(plane_b_sent)
    plane_ref[...] = total_of(plane_b[...], [plane_b_in[d] for d in range(nx - 1)])

    core.finish(0)

    far_sent = [
        remote("bx", col_near.at[lax.rem(pair + d, half)], col_far_in.at[d - 1], 2 * lax.rem(pair + d, half) + odd)
        for d in range(1, half)
    ]

    @pl.when(uneven)
    def _():
        for d in range(1, half + 1):
            to = lax.rem(pair + d, half)
            near_sent[d - 1].wait_recv()
            col_near[to] = col_b[to, 1] + col_near_in[to]
            if d < half:
                far_sent[d - 1].start()

    for h in range(1, chunks):
        core.finish(h)

    @pl.when(even)
    def _():
        home_sent.wait_recv()
        col_ref[...] = col_c[...] + col_c_in[...]
        for copy in near_sent:
            copy.wait_send()

    @pl.when(uneven)
    def _():
        arrived(far_sent)
        col_ref[...] = total_of(col_near[pair], [col_far_in[d] for d in range(half - 1)])
        for copy in [home_sent] + far_sent:
            copy.wait_send()

    arrived(core.full)
    for copy in copies:
        if all(copy is not one for one in near_sent + [home_sent] + far_sent):
            copy.wait_send()


def core_kernel(
    planes_ref, gathered_ref, row_in, col_in, plane_in,
    row_ref, col_ref, plane_ref, out_ref,
    slots, out_sem, small_sem,
):
    count, rows = slots.shape[:2]
    steps = out_ref.shape[0] // rows
    planes, chunks, _, wide = gathered_ref.shape
    small = [
        pltpu.make_async_copy(source, target, small_sem.at[n])
        for n, (source, target) in enumerate(((row_in, row_ref), (col_in, col_ref), (plane_in, plane_ref)))
    ]

    def copy(step, slot):
        return pltpu.make_async_copy(
            slots.at[slot], out_ref.at[pl.ds(step * rows, rows)], out_sem.at[slot]
        )

    def body(step, _):
        slot = lax.rem(step, count)

        @pl.when(step >= count)
        def _():
            copy(step - count, slot).wait()

        for c in range(rows):
            row = step * rows + c
            value = [planes_ref[p, pl.ds(row, 1), :] for p in range(planes)]
            for h in range(chunks):
                total = value[0] * gathered_ref[0, h]
                for p in range(1, planes):
                    total = total + value[p] * gathered_ref[p, h]
                slots[slot, c, :, h * wide:(h + 1) * wide] = total
        copy(step, slot).start()
        return 0

    for one in small:
        one.start()
    lax.fori_loop(0, steps, body, 0)
    for step in range(steps - count, steps):
        copy(step, step % count).wait()
    for one in small:
        one.wait()


def on_device(nx, ny, nz, slab, plane_test, row_test, col_test, core_planes, core_rows, core_cols):
    rank = row_test.shape[1]
    ni, nj = slab.shape[1:]
    ab, bb = core_rows.shape[0] // nx, core_cols.shape[0] // ny
    rb, cb = rank // (ny * nz), rank // (nx * nz)
    half = nx // 2
    wide = 128
    chunks = bb // wide
    depth, planes = core_planes.shape
    shape = lambda *dims: jax.ShapeDtypeStruct(dims, F32)
    vmem = lambda *dims: pltpu.VMEM(dims, F32)
    inputs = (
        slab, plane_test, row_test, col_test, core_planes.T,
        core_rows.reshape(half, 2, ab, ni), core_cols,
    )
    transfers = half + 4 * (nz + ny + nx) + chunks * (nz + 2 * PIECES * ny + half + 4)
    gathered, row_t, plane_sketch, planes_wide, col_t = pl.pallas_call(
        functools.partial(exchange_kernel, nx, ny, nz),
        out_shape=(
            shape(nz, chunks, ab, wide), shape(rb, ni), shape(1, rank), shape(planes, depth, 128),
            shape(cb, nj),
        ),
        in_specs=[pl.BlockSpec(memory_space=pltpu.HBM)] * 7,
        out_specs=[pl.BlockSpec(memory_space=pltpu.VMEM)] * 5,
        scratch_shapes=[
            vmem(1, ni, nj), vmem(1, rank), vmem(ni, rank), vmem(nj, rank), vmem(planes, depth),
            vmem(half, ab, 2 * ni), vmem(chunks, ny * wide, nj),
            vmem(ny, chunks, ni, wide), vmem(ny - 1, chunks, ni, wide),
            vmem(chunks, 2, ni, wide),
            vmem(half, chunks, ab, wide), vmem(half - 1, chunks, ab, wide),
            vmem(nz, ny, rb, ni), vmem(nz - 1, ny, rb, ni),
            vmem(ny, rb, ni), vmem(ny - 1, rb, ni),
            vmem(nz, half, 2, cb, nj), vmem(nz - 1, half, 2, cb, nj),
            vmem(half, 2, cb, nj), vmem(half - 1, cb, nj), vmem(cb, nj), vmem(cb, nj),
            vmem(half, cb, nj), vmem(half, cb, nj), vmem(half - 1, cb, nj),
            vmem(1, rank), vmem(ny - 1, 1, rank),
            vmem(1, rank), vmem(nx - 1, 1, rank),
            pltpu.SemaphoreType.DMA((transfers,)),
            pltpu.SemaphoreType.DMA((transfers,)),
            pltpu.SemaphoreType.DMA((7 + chunks * ny,)),
        ],
        compiler_params=pltpu.CompilerParams(
            collective_id=0, has_side_effects=True, vmem_limit_bytes=32 << 20
        ),
        name="exchange",
    )(*(pltpu.with_memory_space_constraint(a, pltpu.HBM) for a in inputs))
    rows = min(depth, max(1, (1 << 16) // (ab * bb)))
    slots = min(24, depth // rows)
    row_t, col_t, plane_sketch, core_sketch = pl.pallas_call(
        core_kernel,
        out_shape=(shape(rb, ni), shape(cb, nj), shape(1, rank), shape(depth, ab, bb)),
        in_specs=[pl.BlockSpec(memory_space=pltpu.VMEM)] * 5,
        out_specs=[pl.BlockSpec(memory_space=pltpu.HBM)] * 4,
        scratch_shapes=[
            vmem(slots, rows, ab, bb),
            pltpu.SemaphoreType.DMA((slots,)),
            pltpu.SemaphoreType.DMA((3,)),
        ],
        compiler_params=pltpu.CompilerParams(vmem_limit_bytes=16 << 20),
        cost_estimate=pl.CostEstimate(flops=3 * depth * ab * bb, bytes_accessed=4 * depth * ab * bb, transcendentals=0),
        name="core",
    )(planes_wide, gathered, row_t, col_t, plane_sketch)
    return plane_sketch, row_t.T, col_t.T, core_sketch


def solution(mesh):
    in_specs = (
        P(("groups", "bz"), "bx", "by"),
        P("bz", None),
        P("bx", None),
        P("by", None),
        P("bz", None),
        P(None, "bx"),
        P(None, "by"),
    )
    out_specs = (
        P(("groups", "bz"), None),
        P(("groups", "bx"), ("by", "bz")),
        P(("groups", "by"), ("bx", "bz")),
        P(("groups", "bz"), "bx", "by"),
    )
    sizes = [mesh.shape[name] for name in ("bx", "by", "bz")]
    return jax.shard_map(
        functools.partial(on_device, *sizes),
        mesh=mesh, in_specs=in_specs, out_specs=out_specs, check_vma=False,
    )
```
